512 devices in a mesh: tm: 32 (over y_lo, z), fsdp: 16 (over x, y_hi, core).
Axes of the slice: x: 4, y: 8 (y_hi: 2, y_lo: 4; y = y_hi * 4 + y_lo), z: 8, core: 2. Of those that a mesh axis runs over, the one named last changes fastest.
Arguments:
- queries: bfloat16 [128, 512, 12, 128], P('tm', 'fsdp'), may hold values from -5 to 5
- key_states: bfloat16 [128, 512, 12, 128], P('tm', 'fsdp'), may hold values from -5 to 5
- value_states: bfloat16 [128, 512, 12, 128], P('tm', 'fsdp'), may hold values from -6 to 6
- out_grad: bfloat16 [128, 512, 3072], P('tm', 'fsdp'), may hold values from -6 to 6
- out_proj: bfloat16 [1536, 3072], P('fsdp'), may hold values from -0.109375 to 0.109375
Outputs:
- query_grad: bfloat16 [128, 512, 12, 128], P('tm', 'fsdp')
- key_grad: bfloat16 [128, 512, 12, 128], P('tm', 'fsdp')
- value_grad: bfloat16 [128, 512, 12, 128], P('tm', 'fsdp')
The draws below stay inside these ranges and needn't reach their ends.
All inputs are finite; a program needn't handle non-finite values.
Results may differ from the reference program's by a relative error of at most 0.03.
Values may be sent and summed in bfloat16 or wider, within the bound.
A program may use at most 64 MiB of HBM per device.

```python
import math
import jax
import jax.numpy as jnp
from jax import lax

D = 3072
HEADS = 12
HEAD = 128
INNER = 1536
FRAMES = 128
POSITIONS = 512


def draw_queries(key, part):
    own = jax.random.fold_in(key, 1)
    shape = (FRAMES, POSITIONS, HEADS, HEAD)
    values = jnp.clip(jax.random.normal(own, shape, jnp.float32), -4.0, 4.0)
    return values.astype(jnp.bfloat16)


def draw_key_states(key, part):
    own = jax.random.fold_in(key, 2)
    shape = (FRAMES, POSITIONS, HEADS, HEAD)
    values = jnp.clip(jax.random.normal(own, shape, jnp.float32), -4.0, 4.0)
    return values.astype(jnp.bfloat16)


def steps_of(rng, shape, pieces, low, top_value):
    def one(position, shards_of):
        draws = jax.random.uniform(jax.random.fold_in(jax.random.fold_in(rng, 6), position), (shards_of,), jnp.float32, low / len(pieces), top_value / len(pieces))
        return jnp.repeat(jnp.exp(draws), shape[position] // shards_of).reshape((-1,) + (1,) * (len(shape) - position - 1))

    level = one(*pieces[0])
    for cut in pieces[1:]:
        level = level * one(*cut)
    return level


def bell_draw(stream_key, dims, scale, bound, cuts=(), dtype=jnp.bfloat16):
    gain = steps_of(stream_key, dims, cuts, -0.22, 0.18) if cuts else 1.0
    result = jax.random.normal(stream_key, dims, jnp.float32) * scale * gain
    return jnp.minimum(jnp.maximum(result, -bound), bound).astype(dtype)


def setup_inputs(seed: int = 0) -> dict:
    seeds = jax.random.split(jax.random.key(seed), 6)
    return {
        "queries": draw_queries(jax.random.fold_in(seeds[5], 71), 0),
        "key_states": draw_key_states(jax.random.fold_in(seeds[5], 71), 0),
        "value_states": bell_draw(seeds[2], (FRAMES, POSITIONS, HEADS, HEAD), 1.0, 6.0, ((0, 32), (1, 16))),
        "out_grad": bell_draw(seeds[3], (FRAMES, POSITIONS, D), 1.0, 6.0, ((0, 32), (1, 16))),
        "out_proj": bell_draw(seeds[4], (INNER, D), D ** -0.5, 0.109375, ((0, 16),)),
    }


def attend_back(query_block, key_block, value_block, grad_block):
    score_scale = HEAD ** -0.5
    query_wide = query_block.astype(jnp.float32)
    key_wide = key_block.astype(jnp.float32)
    value_wide = value_block.astype(jnp.float32)
    grad_wide = grad_block.astype(jnp.float32)
    scores = jnp.einsum("fphd,gphd->phfg", query_wide, key_wide) * score_scale
    peak = jnp.max(scores, axis=-1, keepdims=True)
    expo = jnp.exp(scores - peak)
    probs = expo / jnp.sum(expo, axis=-1, keepdims=True)
    probs_b = probs.astype(jnp.bfloat16)
    probs_wide = probs_b.astype(jnp.float32)
    attn_out = jnp.einsum("phfg,gphd->fphd", probs_wide, value_wide)
    row_delta = jnp.einsum("fphd,fphd->phf", grad_wide, attn_out)
    dprobs = jnp.einsum("fphd,gphd->phfg", grad_wide, value_wide)
    dscores = (probs * (dprobs - row_delta[..., None])).astype(jnp.bfloat16).astype(jnp.float32)
    query_grad = (jnp.einsum("phfg,gphd->fphd", dscores, key_wide) * score_scale).astype(jnp.bfloat16)
    key_grad = (jnp.einsum("phfg,fphd->gphd", dscores, query_wide) * score_scale).astype(jnp.bfloat16)
    value_grad = jnp.einsum("phfg,fphd->gphd", probs_wide, grad_wide).astype(jnp.bfloat16)
    return query_grad, key_grad, value_grad


def reference(queries, key_states, value_states, out_grad, out_proj):
    flat = out_grad.reshape(FRAMES * POSITIONS, D)
    grad_attn = jnp.dot(flat, out_proj.T, preferred_element_type=jnp.float32).astype(jnp.bfloat16)
    grad_attn = grad_attn.reshape(FRAMES, POSITIONS, HEADS, HEAD)
    block = math.gcd(POSITIONS, 16)
    count = POSITIONS // block

    def split_blocks(array):
        return jnp.transpose(array.reshape(FRAMES, count, block, HEADS, HEAD), (1, 0, 2, 3, 4))

    def join_blocks(array):
        return jnp.transpose(array, (1, 0, 2, 3, 4)).reshape(FRAMES, POSITIONS, HEADS, HEAD)

    def one_block(items):
        return attend_back(items[0], items[1], items[2], items[3])

    outputs = lax.map(one_block, (split_blocks(queries), split_blocks(key_states), split_blocks(value_states), split_blocks(grad_attn)))
    return join_blocks(outputs[0]), join_blocks(outputs[1]), join_blocks(outputs[2])
```

```python
import jax
import jax.numpy as jnp
from jax import lax
from jax.experimental import pallas as pl
from jax.experimental.pallas import tpu as pltpu
from jax.sharding import PartitionSpec as P

MESH = pl.DeviceIdType.MESH
F32 = jnp.float32
BF16 = jnp.bfloat16

NX, NYH, NC = 4, 2, 2
NYL, NZ = 4, 8
NT = NYL * NZ

OWN_O, OWN_E, L_O, L_E, R_O, R_E, D_O, D_E = range(8)


def mm(a, b, ca, cb):
    return lax.dot_general(a, b, (((ca,), (cb,)), ((), ())), preferred_element_type=F32)


def kernel(q_ref, k_ref, v_ref, x_ref, w_ref, dq_ref, dk_ref, dv_ref,
           wbuf, xp, snd, rcv, gs, gr, os, orr,
           own_sem, w_recv, w_recv2, sib_recv, sib_send, w_send,
           qkv_s, qkv_r, g_s, g_r, o_s, o_r):
    t = lax.axis_index("tm")
    f = lax.axis_index("fsdp")
    yl, z = t // NZ, t % NZ
    x, yh, c = f // (NYH * NC), (f // NC) % NYH, f % NC
    heads = q_ref.shape[1]
    frames, pos = x_ref.shape[0], x_ref.shape[1]
    rows = frames * pos
    group = heads // NX
    wrows = w_ref.shape[0]
    half = wrows // 2
    scale = q_ref.shape[-1] ** (-0.5)

    def fs(xx, yy, cc):
        return xx * (NYH * NC) + yy * NC + cc

    right, left, far = (x + 1) % NX, (x + NX - 1) % NX, (x + 2) % NX
    sib = (t, fs(x, yh, 1 - c))
    to_right = (t, fs(right, yh, c))
    to_left = (t, fs(left, yh, c))
    mirror = ((NYL - 1 - yl) * NZ + z, fs(x, 1 - yh, c))
    edge = jnp.logical_or(yl == 0, yl == NYL - 1)
    inner = (jnp.where(yl == 0, 1, NYL - 2) * NZ + z, f)

    def peer(d):
        return ((yl + d % NYL) % NYL) * NZ + (z + 5 * (d // NYL)) % NZ

    barrier = pltpu.get_barrier_semaphore()

    @pl.loop(1, NT)
    def _(d):
        pl.semaphore_signal(barrier, inc=1, device_id=(peer(d), f), device_id_type=MESH)

    for other in (sib, to_right, to_left, mirror):
        pl.semaphore_signal(barrier, inc=1, device_id=other, device_id_type=MESH)
    pl.semaphore_wait(barrier, NT - 1 + 4)

    def block(xx, yy, first=0, count=wrows):
        start = pl.multiple_of((yy * NC + c) * wrows + first, 16)
        return wbuf.at[xx, pl.ds(start, count), :]

    def sib_block(xx, yy):
        start = pl.multiple_of((yy * NC + 1 - c) * wrows, 16)
        return wbuf.at[xx, pl.ds(start, wrows), :]

    def rcopy(src, dst, ssem, rsem, dev):
        return pltpu.make_async_remote_copy(
            src_ref=src, dst_ref=dst, send_sem=ssem, recv_sem=rsem,
            device_id=dev, device_id_type=MESH)

    def arrived(ref, sem):
        pltpu.make_async_copy(ref, ref, sem).wait()

    sent = []

    def send(src, dst, ssem, rsem, dev):
        cp = rcopy(src, dst, ssem, rsem, dev)
        cp.start()
        sent.append(cp)

    own_o = block(x, yh)
    own_copy = pltpu.make_async_copy(w_ref, own_o, own_sem)
    own_copy.start()
    send(w_ref, own_o, w_send.at[0], w_recv.at[L_O], to_right)
    send(w_ref, own_o, w_send.at[1], w_recv.at[R_O], to_left)
    send(w_ref, own_o, sib_send.at[OWN_O], sib_recv.at[OWN_O], sib)
    to_mirror = [
        rcopy(w_ref.at[pl.ds(i * half, half), :], block(x, yh, i * half, half),
              w_send.at[2 + i], w_recv2.at[i], mirror)
        for i in range(2)
    ]

    @pl.when(edge)
    def _():
        for cp in to_mirror:
            cp.start()

    ri = lax.broadcasted_iota(jnp.int32, (rows, rows), 0)
    ci = lax.broadcasted_iota(jnp.int32, (rows, rows), 1)
    to_pos = ((ri % frames) * pos + ri // frames == ci).astype(F32).astype(BF16)
    to_frame = ((ri % pos) * frames + ri // pos == ci).astype(F32).astype(BF16)

    snd_v = snd.reshape(3, heads, rows, 128)
    rcv_v = rcv.reshape(3, heads, 128, 128)
    gs_v = gs.reshape(heads, rows, 128)
    gr_v = gr.reshape(heads, 128, 128)
    os_v = os.reshape(3, heads, 128, 128)
    orr_v = orr.reshape(3, heads, rows, 128)

    @pl.loop(0, heads)
    def _(h):
        for i, ref in enumerate((q_ref, k_ref, v_ref)):
            snd_v[i, h] = mm(to_pos, ref[:, h].reshape(rows, 128), 1, 0).astype(BF16)

    pltpu.make_async_copy(snd.at[:, :, t], rcv.at[:, :, t], qkv_r).start()

    @pl.loop(1, NT)
    def _(d):
        p = peer(d)
        rcopy(snd.at[:, :, p], rcv.at[:, :, t], qkv_s, qkv_r, (p, f)).start()

    @pl.loop(0, x_ref.shape[2] // 512)
    def _(i):
        cols = pl.ds(pl.multiple_of(i * 512, 512), 512)
        xp[:, cols] = mm(to_pos, x_ref[:, :, cols].reshape(rows, 512), 1, 0).astype(BF16)

    def share(which, xx, yy):
        send(block(xx, yy), block(xx, yy), sib_send.at[which], sib_recv.at[which], sib)

    arrived(block(left, yh), w_recv.at[L_O])
    send(block(left, yh, 0, half), block(left, yh, 0, half), w_send.at[4], w_recv.at[D_O], to_right)
    share(L_O, left, yh)
    arrived(block(right, yh), w_recv.at[R_O])
    send(block(right, yh, half, half), block(right, yh, half, half), w_send.at[5], w_recv2.at[2], to_left)
    share(R_O, right, yh)

    oh = 1 - yh
    to_inner = [
        rcopy(block(x, oh, i * half, half), block(x, oh, i * half, half),
              w_send.at[6 + i], w_recv2.at[i], inner)
        for i in range(2)
    ]
    for i in range(2):
        arrived(block(x, oh, i * half, half), w_recv2.at[i])

        @pl.when(edge)
        def _():
            to_inner[i].start()

    send(block(x, oh), block(x, oh), w_send.at[8], w_recv.at[L_E], to_right)
    send(block(x, oh), block(x, oh), w_send.at[9], w_recv.at[R_E], to_left)
    share(OWN_E, x, oh)

    def project(xx):
        acc = mm(xp[...], wbuf[xx], 1, 1)
        for i in range(group):
            gs_v[xx * group + i] = acc[:, i * 128:(i + 1) * 128].astype(BF16)

    def send_g(step, xx):
        hs = pl.ds(xx * group, group)
        pltpu.make_async_copy(gs.at[hs, t], gr.at[hs, t], g_r.at[step]).start()

        @pl.loop(1, NT)
        def _(d):
            p = peer(d)
            rcopy(gs.at[hs, p], gr.at[hs, t], g_s.at[step], g_r.at[step], (p, f)).start()

    def attend(step, xx):
        hs = pl.ds(xx * group, group)
        arrived(gr.at[hs], g_r.at[step])
        for i in range(group):
            h = xx * group + i
            q, k, v, g = rcv_v[0, h], rcv_v[1, h], rcv_v[2, h], gr_v[h]
            s = mm(k, q, 1, 1) * scale
            e = jnp.exp(s - jnp.max(s, axis=0, keepdims=True))
            probs = e * (1.0 / jnp.sum(e, axis=0, keepdims=True))
            pb = probs.astype(BF16)
            dp = mm(v, g, 1, 1)
            delta = jnp.sum(pb.astype(F32) * dp, axis=0, keepdims=True)
            ds = (probs * (dp - delta)).astype(BF16)
            os_v[0, h] = (mm(ds, k, 0, 0) * scale).astype(BF16)
            os_v[1, h] = (mm(ds, q, 1, 0) * scale).astype(BF16)
            os_v[2, h] = mm(pb, g, 1, 0).astype(BF16)
        pltpu.make_async_copy(os.at[:, hs, t], orr.at[:, hs, t], o_r.at[step]).start()

        @pl.loop(1, NT)
        def _(d):
            p = peer(d)
            rcopy(os.at[:, hs, p], orr.at[:, hs, t], o_s.at[step], o_r.at[step], (p, f)).start()

    def finish(step, xx):
        hs = pl.ds(xx * group, group)
        arrived(orr.at[:, hs], o_r.at[step])
        for j, ref in enumerate((dq_ref, dk_ref, dv_ref)):
            for i in range(group):
                h = xx * group + i
                ref[:, h] = mm(to_frame, orr_v[j, h], 1, 0).astype(BF16).reshape(frames, pos, 128)

    own_copy.wait()
    arrived(sib_block(x, yh), sib_recv.at[OWN_O])
    arrived(sib_block(x, oh), sib_recv.at[OWN_E])
    project(x)
    send_g(0, x)

    arrived(block(left, oh), w_recv.at[L_E])
    send(block(left, oh, 0, half), block(left, oh, 0, half), w_send.at[10], w_recv.at[D_E], to_right)
    share(L_E, left, oh)
    arrived(block(right, oh), w_recv.at[R_E])
    send(block(right, oh, half, half), block(right, oh, half, half), w_send.at[11], w_recv2.at[3], to_left)
    share(R_E, right, oh)
    arrived(block(far, yh, 0, half), w_recv.at[D_O])
    arrived(block(far, yh, half, half), w_recv2.at[2])
    share(D_O, far, yh)

    arrived(sib_block(right, yh), sib_recv.at[R_O])
    arrived(sib_block(right, oh), sib_recv.at[R_E])
    project(right)
    send_g(1, right)
    arrived(sib_block(left, yh), sib_recv.at[L_O])
    arrived(sib_block(left, oh), sib_recv.at[L_E])
    project(left)
    send_g(2, left)

    arrived(rcv, qkv_r)
    attend(0, x)
    arrived(block(far, oh, 0, half), w_recv.at[D_E])
    arrived(block(far, oh, half, half), w_recv2.at[3])
    share(D_E, far, oh)
    attend(1, right)
    arrived(sib_block(far, yh), sib_recv.at[D_O])
    arrived(sib_block(far, oh), sib_recv.at[D_E])
    project(far)
    send_g(3, far)
    attend(2, left)
    attend(3, far)

    for step, xx in enumerate((x, right, left, far)):
        finish(step, xx)

    for cp in sent:
        cp.wait_send()

    @pl.when(edge)
    def _():
        for cp in to_mirror + to_inner:
            cp.wait_send()

    rest = snd.at[:, :, pl.ds(0, NT - 1)]
    pltpu.make_async_copy(rest, rest, qkv_s).wait()
    for step, xx in enumerate((x, right, left, far)):
        hs = pl.ds(xx * group, group)
        rest = gs.at[hs, pl.ds(0, NT - 1)]
        pltpu.make_async_copy(rest, rest, g_s.at[step]).wait()
        rest = os.at[:, hs, pl.ds(0, NT - 1)]
        pltpu.make_async_copy(rest, rest, o_s.at[step]).wait()


def body(queries, key_states, value_states, out_grad, out_proj):
    frames, pos, heads, size = queries.shape
    wrows, width = out_proj.shape
    vmem = pl.BlockSpec(memory_space=pltpu.VMEM)
    dma = pltpu.SemaphoreType.DMA

    def turn(a):
        return jnp.transpose(a, (0, 2, 1, 3))

    outs = pl.pallas_call(
        kernel,
        out_shape=[jax.ShapeDtypeStruct((frames, heads, pos, size), BF16)] * 3,
        in_specs=[vmem] * 5,
        out_specs=[vmem] * 3,
        scratch_shapes=[
            pltpu.VMEM((NX, NYH * NC * wrows, width), BF16),
            pltpu.VMEM((frames * pos, width), BF16),
            pltpu.VMEM((3, heads, pos, frames, size), BF16),
            pltpu.VMEM((3, heads, NT, frames, size), BF16),
            pltpu.VMEM((heads, pos, frames, size), BF16),
            pltpu.VMEM((heads, NT, frames, size), BF16),
            pltpu.VMEM((3, heads, NT, frames, size), BF16),
            pltpu.VMEM((3, heads, pos, frames, size), BF16),
            dma, dma((8,)), dma((4,)), dma((8,)), dma((8,)), dma((12,)),
            dma, dma, dma((4,)), dma((4,)), dma((4,)), dma((4,)),
        ],
        compiler_params=pltpu.CompilerParams(
            collective_id=0, has_side_effects=True, vmem_limit_bytes=48 << 20),
    )(turn(queries), turn(key_states), turn(value_states), out_grad, out_proj)
    return tuple(turn(o) for o in outs)


def solution(mesh):
    return jax.shard_map(
        body,
        mesh=mesh,
        in_specs=(
            P("tm", "fsdp", None, None),
            P("tm", "fsdp", None, None),
            P("tm", "fsdp", None, None),
            P("tm", "fsdp", None),
            P("fsdp", None),
        ),
        out_specs=(
            P("tm", "fsdp", None, None),
            P("tm", "fsdp", None, None),
            P("tm", "fsdp", None, None),
        ),
        check_vma=False,
    )
```

```python
import jax
import jax.numpy as jnp
from jax import lax
from jax.experimental import pallas as pl
from jax.experimental.pallas import tpu as pltpu
from jax.sharding import PartitionSpec as P

MESH = pl.DeviceIdType.MESH
F32 = jnp.float32
BF16 = jnp.bfloat16

NX, NYH, NC = 4, 2, 2
NYL, NZ = 4, 8
NT = NYL * NZ

NE = 6


def mm(a, b, ca, cb):
    return lax.dot_general(a, b, (((ca,), (cb,)), ((), ())), preferred_element_type=F32)


def kernel(q_ref, k_ref, v_ref, x_ref, w_ref, dq_ref, dk_ref, dv_ref,
           qin, wbuf, xbuf, snd, rcv, gst_a, gs_a, gr_a, os_a, or_a, gst_b, gs_b, gr_b, os_b, or_b, out,
           in_sem, w_send, sib_send, sib_recv, e_recv, x_send, x_recv, xh_recv,
           gx_send, gx_recv, out_sem, qkv_s, qkv_r, g_s, g_r, o_s, o_r):
    t = lax.axis_index("tm")
    f = lax.axis_index("fsdp")
    yl, z = t // NZ, t % NZ
    x, yh, c = f // (NYH * NC), (f // NC) % NYH, f % NC
    frames, heads, pos, size = q_ref.shape
    rows = frames * pos
    group = heads // NX
    wrows = w_ref.shape[0]
    part = wrows // NE
    scale = size ** (-0.5)

    def fs(xx, yy, cc):
        return xx * (NYH * NC) + yy * NC + cc

    right, left, far = (x + 1) % NX, (x + NX - 1) % NX, (x + 2) % NX
    oh = 1 - yh
    sib = (t, fs(x, yh, 1 - c))

    def along_x(xx):
        return (t, fs(xx, yh, c))

    mirror = ((NYL - 1 - yl) * NZ + z, fs(x, oh, c))
    edge = jnp.logical_or(yl == 0, yl == NYL - 1)
    inner = (jnp.where(yl == 0, 1, NYL - 2) * NZ + z, f)

    def peer(d):
        return ((yl + d // NZ) % NYL) * NZ + (z + 5 * (d % NZ)) % NZ

    def block(yy, cc, i=0, n=NE):
        start = pl.multiple_of((yy * NC + cc) * wrows + i * part, 8)
        return wbuf.at[pl.ds(start, n * part), :]

    loads = [pltpu.make_async_copy(src, qin.at[i], in_sem.at[i])
             for i, src in enumerate((q_ref, k_ref, v_ref))]
    loads.append(pltpu.make_async_copy(w_ref, block(yh, c), in_sem.at[3]))
    loads.append(pltpu.make_async_copy(x_ref, xbuf.at[x], in_sem.at[4]))
    for cp in loads:
        cp.start()

    barrier = pltpu.get_barrier_semaphore()

    @pl.loop(1, NT)
    def _(d):
        pl.semaphore_signal(barrier, inc=1, device_id=(peer(d), f), device_id_type=MESH)

    others = (sib, along_x(right), along_x(left), along_x(far), mirror)
    for other in others:
        pl.semaphore_signal(barrier, inc=1, device_id=other, device_id_type=MESH)
    ri = lax.broadcasted_iota(jnp.int32, (rows, rows), 0)
    ci = lax.broadcasted_iota(jnp.int32, (rows, rows), 1)
    to_pos = ((ri % frames) * pos + ri // frames == ci).astype(F32).astype(BF16)
    to_frame = ((ri % pos) * frames + ri // pos == ci).astype(F32).astype(BF16)

    snd_v = snd.reshape(3, heads, rows, size)
    rcv_v = rcv.reshape(3, heads, NT * frames, size)

    for cp in loads[:3]:
        cp.wait()

    @pl.loop(0, heads)
    def _(h):
        for i in range(3):
            snd_v[i, h] = mm(to_pos, qin[i, :, h].reshape(rows, size), 1, 0).astype(BF16)

    pl.semaphore_wait(barrier, NT - 1 + len(others))

    def rcopy(src, dst, ssem, rsem, dev):
        return pltpu.make_async_remote_copy(
            src_ref=src, dst_ref=dst, send_sem=ssem, recv_sem=rsem,
            device_id=dev, device_id_type=MESH)

    def arrived(ref, sem):
        pltpu.make_async_copy(ref, ref, sem).wait()

    sent = []

    def send(src, dst, ssem, rsem, dev):
        cp = rcopy(src, dst, ssem, rsem, dev)
        cp.start()
        sent.append(cp)

    to_mirror = [
        rcopy(w_ref.at[pl.ds(i * part, part), :], block(yh, c, i, 1), w_send.at[i], e_recv.at[i], mirror)
        for i in range(NE)
    ]
    to_inner = [
        rcopy(block(oh, c, i, 1), block(oh, c, i, 1), w_send.at[NE + i], e_recv.at[i], inner)
        for i in range(NE)
    ]
    to_sib = [
        rcopy(block(oh, c, i, 1), block(oh, c, i, 1), sib_send.at[i], sib_recv.at[i], sib)
        for i in range(NE)
    ]

    @pl.when(edge)
    def _():
        for cp in to_mirror:
            cp.start()

    send(x_ref, xbuf.at[x], x_send.at[0], x_recv.at[0], along_x(right))
    send(x_ref, xbuf.at[x], x_send.at[1], x_recv.at[1], along_x(left))
    send(w_ref, block(yh, c), sib_send.at[NE], sib_recv.at[NE], sib)

    pltpu.make_async_copy(snd.at[:, :, t], rcv.at[:, :, t], qkv_r).start()

    @pl.loop(1, NT)
    def _(d):
        p = peer(d)
        rcopy(snd.at[:, :, p], rcv.at[:, :, t], qkv_s, qkv_r, (p, f)).start()

    order = (x, right, left, far)
    first = (group - 1) * yh
    rest = 1 - yh
    nb = group - 1

    class Phase:
        def __init__(self, gst, gs, gr, os, orr, count, head, sems):
            n = NX * count
            self.gst, self.gs, self.gr, self.os, self.orr = gst, gs, gr, os, orr
            self.gst_v = gst.reshape(NX * count, rows, size)
            self.gs_v = gs.reshape(n, rows, size)
            self.gr_v = gr.reshape(n, NT * frames, size)
            self.os_v = os.reshape(3, n, NT * frames, size)
            self.orr_v = orr.reshape(3, n, rows, size)
            self.count, self.head, self.sems = count, head, sems

    pa = Phase(gst_a, gs_a, gr_a, os_a, or_a, 1, first, 0)
    pb = Phase(gst_b, gs_b, gr_b, os_b, or_b, nb, rest, 3)

    def project(ph, xx):
        ws = pl.ds(pl.multiple_of(ph.head * size, size), ph.count * size)
        acc = mm(xbuf[xx].reshape(rows, -1), wbuf[ws, :], 1, 1).astype(BF16)
        return mm(to_pos, acc, 1, 0).astype(BF16)

    def own_g(ph):
        acc = project(ph, x)
        for j in range(ph.count):
            ph.gs_v[j] = acc[:, j * size:(j + 1) * size]

    back = (2, 1, 3)

    def return_g(ph, i):
        xx = order[i + 1]
        acc = project(ph, xx)
        for j in range(ph.count):
            ph.gst_v[i * ph.count + j] = acc[:, j * size:(j + 1) * size]
        send(ph.gst.at[pl.ds(i * ph.count, ph.count)], ph.gs.at[pl.ds(back[i] * ph.count, ph.count)],
             gx_send.at[ph.sems + i], gx_recv.at[ph.sems + back[i] - 1], along_x(xx))

    def take_g(ph, slot):
        arrived(ph.gs.at[pl.ds(slot * ph.count, ph.count)], gx_recv.at[ph.sems + slot - 1])

    steps = []

    def send_g(ph, lo, n):
        step = len(steps)
        hs = pl.ds(lo * ph.count, n * ph.count)
        steps.append((ph, lo, n, hs))
        pltpu.make_async_copy(ph.gs.at[hs, t], ph.gr.at[hs, t], g_r.at[step]).start()

        @pl.loop(1, NT)
        def _(d):
            p = peer(d)
            rcopy(ph.gs.at[hs, p], ph.gr.at[hs, t], g_s.at[step], g_r.at[step], (p, f)).start()

    def attend(step):
        ph, lo, n, hs = steps[step]
        arrived(ph.gr.at[hs], g_r.at[step])
        for i in range(lo, lo + n):
            for j in range(ph.count):
                h, m = order[i] * group + ph.head + j, i * ph.count + j
                q, k, v, g = rcv_v[0, h], rcv_v[1, h], rcv_v[2, h], ph.gr_v[m]
                s = mm(k, q, 1, 1) * scale
                e = jnp.exp(s - jnp.max(s, axis=0, keepdims=True))
                probs = e * (1.0 / jnp.sum(e, axis=0, keepdims=True))
                pb16 = probs.astype(BF16)
                dp = mm(v, g, 1, 1)
                delta = jnp.sum(pb16.astype(F32) * dp, axis=0, keepdims=True)
                ds = (probs * (dp - delta)).astype(BF16)
                ph.os_v[0, m] = (mm(ds, k, 0, 0) * scale).astype(BF16)
                ph.os_v[1, m] = (mm(ds, q, 1, 0) * scale).astype(BF16)
                ph.os_v[2, m] = mm(pb16, g, 1, 0).astype(BF16)
        pltpu.make_async_copy(ph.os.at[:, hs, t], ph.orr.at[:, hs, t], o_r.at[step]).start()

        @pl.loop(1, NT)
        def _(d):
            p = peer(d)
            rcopy(ph.os.at[:, hs, p], ph.orr.at[:, hs, t], o_s.at[step], o_r.at[step], (p, f)).start()

    stores = []

    def finish(step):
        ph, lo, n, hs = steps[step]
        arrived(ph.orr.at[:, hs], o_r.at[step])
        for j, ref in enumerate((dq_ref, dk_ref, dv_ref)):
            for i in range(lo, lo + n):
                start = order[i] * group + ph.head
                for u in range(ph.count):
                    out[j, :, start + u] = mm(to_frame, ph.orr_v[j, i * ph.count + u], 1, 0).astype(BF16).reshape(
                        frames, pos, size)
                cp = pltpu.make_async_copy(out.at[j, :, pl.ds(start, ph.count)], ref.at[:, pl.ds(start, ph.count)],
                                           out_sem.at[len(stores)])
                cp.start()
                stores.append(cp)

    loads[3].wait()
    loads[4].wait()
    arrived(block(yh, 1 - c), sib_recv.at[NE])
    own_g(pa)

    @pl.when(edge)
    def _():
        for i in range(NE):
            arrived(block(oh, c, i, 1), e_recv.at[i])
            to_inner[i].start()
            to_sib[i].start()

    hf = frames // 2
    arrived(xbuf.at[left], x_recv.at[0])
    low = xbuf.at[left, pl.ds(0, hf)]
    send(low, low, x_send.at[2], xh_recv.at[0], along_x(right))
    arrived(xbuf.at[right], x_recv.at[1])
    high = xbuf.at[right, pl.ds(hf, hf)]
    send(high, high, x_send.at[3], xh_recv.at[1], along_x(left))
    return_g(pa, 0)
    return_g(pa, 1)
    arrived(xbuf.at[far, pl.ds(0, hf)], xh_recv.at[0])
    arrived(xbuf.at[far, pl.ds(hf, hf)], xh_recv.at[1])
    return_g(pa, 2)

    @pl.when(jnp.logical_not(edge))
    def _():
        for i in range(NE):
            arrived(block(oh, c, i, 1), e_recv.at[i])
            to_sib[i].start()

    for slot in (1, 2, 3):
        take_g(pa, slot)
    send_g(pa, 0, 4)

    for i in range(NE):
        arrived(block(oh, 1 - c, i, 1), sib_recv.at[i])
    for i in range(3):
        return_g(pb, i)
    own_g(pb)
    take_g(pb, 1)
    send_g(pb, 0, 2)
    take_g(pb, 2)
    take_g(pb, 3)
    send_g(pb, 2, 2)

    arrived(rcv, qkv_r)
    for step in range(3):
        attend(step)
    for step in range(3):
        finish(step)
    for cp in stores:
        cp.wait()

    for cp in sent + to_sib:
        cp.wait_send()

    @pl.when(edge)
    def _():
        for cp in to_mirror + to_inner:
            cp.wait_send()

    others = snd.at[:, :, pl.ds(0, NT - 1)]
    pltpu.make_async_copy(others, others, qkv_s).wait()
    for step, (ph, lo, n, hs) in enumerate(steps):
        others = ph.gs.at[hs, pl.ds(0, NT - 1)]
        pltpu.make_async_copy(others, others, g_s.at[step]).wait()
        others = ph.os.at[:, hs, pl.ds(0, NT - 1)]
        pltpu.make_async_copy(others, others, o_s.at[step]).wait()


def body(queries, key_states, value_states, out_grad, out_proj):
    frames, pos, heads, size = queries.shape
    wrows, width = out_proj.shape
    hbm = pl.BlockSpec(memory_space=pltpu.HBM)
    dma = pltpu.SemaphoreType.DMA

    def turn(a):
        return jnp.transpose(a, (0, 2, 1, 3))

    def phase(count):
        n = NX * count
        return [pltpu.VMEM(shape, BF16) for shape in (
            (n, pos, frames, size), (n, pos, frames, size), (n, NT, frames, size),
            (3, n, NT, frames, size), (3, n, pos, frames, size))]

    outs = pl.pallas_call(
        kernel,
        out_shape=[jax.ShapeDtypeStruct((frames, heads, pos, size), BF16)] * 3,
        in_specs=[hbm] * 5,
        out_specs=[hbm] * 3,
        scratch_shapes=[
            pltpu.VMEM((3, frames, heads, pos, size), BF16),
            pltpu.VMEM((NYH * NC * wrows, width), BF16),
            pltpu.VMEM((NX, frames, pos, width), BF16),
            pltpu.VMEM((3, heads, pos, frames, size), BF16),
            pltpu.VMEM((3, heads, NT, frames, size), BF16),
            *phase(1),
            *phase(heads // NX - 1),
            pltpu.VMEM((3, frames, heads, pos, size), BF16),
            dma((5,)), dma((2 * NE,)), dma((NE + 1,)), dma((NE + 1,)), dma((NE,)),
            dma((4,)), dma((2,)), dma((2,)), dma((6,)), dma((6,)), dma((3 * heads,)),
            dma, dma, dma((3,)), dma((3,)), dma((3,)), dma((3,)),
        ],
        compiler_params=pltpu.CompilerParams(
            collective_id=0, has_side_effects=True, vmem_limit_bytes=60 << 20),
    )(turn(queries), turn(key_states), turn(value_states), out_grad, out_proj)
    return tuple(turn(o) for o in outs)


def solution(mesh):
    return jax.shard_map(
        body,
        mesh=mesh,
        in_specs=(
            P("tm", "fsdp", None, None),
            P("tm", "fsdp", None, None),
            P("tm", "fsdp", None, None),
            P("tm", "fsdp", None),
            P("fsdp", None),
        ),
        out_specs=(
            P("tm", "fsdp", None, None),
            P("tm", "fsdp", None, None),
            P("tm", "fsdp", None, None),
        ),
        check_vma=False,
    )
```

```python
import jax
import jax.numpy as jnp
from jax import lax
from jax.experimental import pallas as pl
from jax.experimental.pallas import tpu as pltpu
from jax.sharding import PartitionSpec as P

MESH = pl.DeviceIdType.MESH
F32 = jnp.float32
BF16 = jnp.bfloat16

NX, NYH, NC = 4, 2, 2
NYL, NZ = 4, 8
NT = NYL * NZ

NE = 6


def mm(a, b, ca, cb):
    return lax.dot_general(a, b, (((ca,), (cb,)), ((), ())), preferred_element_type=F32)


def kernel(q_ref, k_ref, v_ref, x_ref, w_ref, dq_ref, dk_ref, dv_ref,
           qin, wbuf, xbuf, snd, rcv, gst_a, gs_a, gr_a, os_a, or_a, out,
           in_sem, w_send, sib_send, sib_recv, e_recv, x_send, x_recv, xh_recv,
           gx_send, gx_recv, out_sem, qkv_s, qkv_r, g_s, g_r, o_s, o_r):
    t = lax.axis_index("tm")
    f = lax.axis_index("fsdp")
    yl, z = t // NZ, t % NZ
    x, yh, c = f // (NYH * NC), (f // NC) % NYH, f % NC
    frames, heads, pos, size = q_ref.shape
    rows = frames * pos
    group = heads // NX
    wrows = w_ref.shape[0]
    part = wrows // NE
    scale = size ** (-0.5)

    def fs(xx, yy, cc):
        return xx * (NYH * NC) + yy * NC + cc

    right, left, far = (x + 1) % NX, (x + NX - 1) % NX, (x + 2) % NX
    oh = 1 - yh
    sib = (t, fs(x, yh, 1 - c))

    def along_x(xx):
        return (t, fs(xx, yh, c))

    mirror = ((NYL - 1 - yl) * NZ + z, fs(x, oh, c))
    edge = jnp.logical_or(yl == 0, yl == NYL - 1)
    inner = (jnp.where(yl == 0, 1, NYL - 2) * NZ + z, f)

    def peer(d):
        away = d - NZ
        dy = jnp.where(d < NZ, 0, 1 + away % (NYL - 1))
        dz = jnp.where(d < NZ, 5 * d, 5 * (away // (NYL - 1)))
        return ((yl + dy) % NYL) * NZ + (z + dz) % NZ

    def block(yy, cc, i=0, n=NE):
        start = pl.multiple_of((yy * NC + cc) * wrows + i * part, 8)
        return wbuf.at[pl.ds(start, n * part), :]

    loads = [pltpu.make_async_copy(src, qin.at[i], in_sem.at[i])
             for i, src in enumerate((q_ref, k_ref, v_ref))]
    loads.append(pltpu.make_async_copy(w_ref, block(yh, c), in_sem.at[3]))
    loads.append(pltpu.make_async_copy(x_ref, xbuf.at[x], in_sem.at[4]))
    for cp in loads:
        cp.start()

    barrier = pltpu.get_barrier_semaphore()

    @pl.loop(1, NT)
    def _(d):
        pl.semaphore_signal(barrier, inc=1, device_id=(peer(d), f), device_id_type=MESH)

    others = (sib, along_x(right), along_x(left), along_x(far), mirror)
    for other in others:
        pl.semaphore_signal(barrier, inc=1, device_id=other, device_id_type=MESH)
    ri = lax.broadcasted_iota(jnp.int32, (rows, rows), 0)
    ci = lax.broadcasted_iota(jnp.int32, (rows, rows), 1)
    to_pos = ((ri % frames) * pos + ri // frames == ci).astype(F32).astype(BF16)
    to_frame = ((ri % pos) * frames + ri // pos == ci).astype(F32).astype(BF16)

    snd_v = snd.reshape(3, heads, rows, size)
    rcv_v = rcv.reshape(3, heads, NT * frames, size)

    for cp in loads[:3]:
        cp.wait()

    order = (x, right, left, far)

    @pl.loop(0, group)
    def _(j):
        for r in range(NX):
            for i in range(3):
                src = qin[i, :, order[r] * group + j].reshape(rows, size)
                snd_v[i, r * group + j] = mm(to_pos, src, 1, 0).astype(BF16)

    pl.semaphore_wait(barrier, NT - 1 + len(others))

    def rcopy(src, dst, ssem, rsem, dev):
        return pltpu.make_async_remote_copy(
            src_ref=src, dst_ref=dst, send_sem=ssem, recv_sem=rsem,
            device_id=dev, device_id_type=MESH)

    def arrived(ref, sem):
        pltpu.make_async_copy(ref, ref, sem).wait()

    sent = []

    def send(src, dst, ssem, rsem, dev):
        cp = rcopy(src, dst, ssem, rsem, dev)
        cp.start()
        sent.append(cp)

    to_mirror = [
        rcopy(w_ref.at[pl.ds(i * part, part), :], block(yh, c, i, 1), w_send.at[i], e_recv.at[i], mirror)
        for i in range(NE)
    ]
    to_inner = [
        rcopy(block(oh, c, i, 1), block(oh, c, i, 1), w_send.at[NE + i], e_recv.at[i], inner)
        for i in range(NE)
    ]
    to_sib = [
        rcopy(block(oh, c, i, 1), block(oh, c, i, 1), sib_send.at[i], sib_recv.at[i], sib)
        for i in range(NE)
    ]

    @pl.when(edge)
    def _():
        for cp in to_mirror:
            cp.start()

    send(x_ref, xbuf.at[x], x_send.at[0], x_recv.at[0], along_x(right))
    send(x_ref, xbuf.at[x], x_send.at[1], x_recv.at[1], along_x(left))
    send(w_ref, block(yh, c), sib_send.at[NE], sib_recv.at[NE], sib)

    parts = (pl.ds(0, group), pl.ds(group, heads - group))
    for i, hs in enumerate(parts):
        pltpu.make_async_copy(snd.at[:, hs, t], rcv.at[:, hs, t], qkv_r.at[i]).start()

    def send_qkv(i, lo, hi):
        hs = parts[i]

        @pl.loop(lo, hi)
        def _(d):
            p = peer(d)
            rcopy(snd.at[:, hs, p], rcv.at[:, hs, t], qkv_s.at[i], qkv_r.at[i], (p, f)).start()

    for i in range(2):
        send_qkv(i, 1, NZ)

    @pl.when(edge)
    def _():
        for i in range(NE):
            arrived(block(oh, c, i, 1), e_recv.at[i])
            to_inner[i].start()
            to_sib[i].start()

    send_qkv(0, NZ, NT)

    @pl.when(jnp.logical_not(edge))
    def _():
        send_qkv(1, NZ, NT)


    class Phase:
        def __init__(self, gst, gs, gr, os, orr, count, head, sems):
            n = NX * count
            self.gst, self.gs, self.gr, self.os, self.orr = gst, gs, gr, os, orr
            self.gst_v = gst.reshape(NX * count, rows, size)
            self.gs_v = gs.reshape(n, rows, size)
            self.gr_v = gr.reshape(n, NT * frames, size)
            self.os_v = os.reshape(3, n, NT * frames, size)
            self.orr_v = orr.reshape(3, n, rows, size)
            self.count, self.head, self.sems = count, head, sems

    pa = Phase(gst_a, gs_a, gr_a, os_a, or_a, group, 0, 0)

    def project(ph, xx):
        acc = mm(xbuf[xx].reshape(rows, -1), wbuf[...], 1, 1).astype(BF16)
        return mm(to_pos, acc, 1, 0).astype(BF16)

    def own_g(ph):
        acc = project(ph, x)
        for j in range(ph.count):
            ph.gs_v[j] = acc[:, j * size:(j + 1) * size]

    back = (2, 1, 3)

    def return_g(ph, i):
        xx = order[i + 1]
        acc = project(ph, xx)
        for j in range(ph.count):
            ph.gst_v[i * ph.count + j] = acc[:, j * size:(j + 1) * size]
        send(ph.gst.at[pl.ds(i * ph.count, ph.count)], ph.gs.at[pl.ds(back[i] * ph.count, ph.count)],
             gx_send.at[ph.sems + i], gx_recv.at[ph.sems + back[i] - 1], along_x(xx))

    def take_g(ph, slot):
        arrived(ph.gs.at[pl.ds(slot * ph.count, ph.count)], gx_recv.at[ph.sems + slot - 1])

    steps = []

    def send_g(ph, lo, n):
        step = len(steps)
        hs = pl.ds(lo * ph.count, n * ph.count)
        steps.append((ph, lo, n, hs))
        pltpu.make_async_copy(ph.gs.at[hs, t], ph.gr.at[hs, t], g_r.at[step]).start()

        @pl.loop(1, NT)
        def _(d):
            p = peer(d)
            rcopy(ph.gs.at[hs, p], ph.gr.at[hs, t], g_s.at[step], g_r.at[step], (p, f)).start()

    def attend(step):
        ph, lo, n, hs = steps[step]
        arrived(ph.gr.at[hs], g_r.at[step])
        for i in range(lo, lo + n):
            for j in range(ph.count):
                h = m = i * ph.count + j
                q, k, v, g = rcv_v[0, h], rcv_v[1, h], rcv_v[2, h], ph.gr_v[m]
                s = mm(k, q, 1, 1) * scale
                e = jnp.exp(s - jnp.max(s, axis=0, keepdims=True))
                probs = e * (1.0 / jnp.sum(e, axis=0, keepdims=True))
                pb16 = probs.astype(BF16)
                dp = mm(v, g, 1, 1)
                delta = jnp.sum(pb16.astype(F32) * dp, axis=0, keepdims=True)
                ds = (probs * (dp - delta)).astype(BF16)
                ph.os_v[0, m] = (mm(ds, k, 0, 0) * scale).astype(BF16)
                ph.os_v[1, m] = (mm(ds, q, 1, 0) * scale).astype(BF16)
                ph.os_v[2, m] = mm(pb16, g, 1, 0).astype(BF16)
        pltpu.make_async_copy(ph.os.at[:, hs, t], ph.orr.at[:, hs, t], o_r.at[step]).start()

        @pl.loop(1, NT)
        def _(d):
            p = peer(d)
            rcopy(ph.os.at[:, hs, p], ph.orr.at[:, hs, t], o_s.at[step], o_r.at[step], (p, f)).start()

    stores = []

    def finish(step):
        ph, lo, n, hs = steps[step]
        arrived(ph.orr.at[:, hs], o_r.at[step])
        for j, ref in enumerate((dq_ref, dk_ref, dv_ref)):
            for i in range(lo, lo + n):
                start = order[i] * group + ph.head
                for u in range(ph.count):
                    out[j, :, start + u] = mm(to_frame, ph.orr_v[j, i * ph.count + u], 1, 0).astype(BF16).reshape(
                        frames, pos, size)
                cp = pltpu.make_async_copy(out.at[j, :, pl.ds(start, ph.count)], ref.at[:, pl.ds(start, ph.count)],
                                           out_sem.at[len(stores)])
                cp.start()
                stores.append(cp)

    @pl.when(jnp.logical_not(edge))
    def _():
        for i in range(NE):
            arrived(block(oh, c, i, 1), e_recv.at[i])
            to_sib[i].start()

    hf = frames // 2
    arrived(xbuf.at[left], x_recv.at[0])
    low = xbuf.at[left, pl.ds(0, hf)]
    send(low, low, x_send.at[2], xh_recv.at[0], along_x(right))
    arrived(xbuf.at[right], x_recv.at[1])
    high = xbuf.at[right, pl.ds(hf, hf)]
    send(high, high, x_send.at[3], xh_recv.at[1], along_x(left))

    loads[3].wait()
    loads[4].wait()
    arrived(block(yh, 1 - c), sib_recv.at[NE])
    for i in range(NE):
        arrived(block(oh, 1 - c, i, 1), sib_recv.at[i])
    return_g(pa, 0)
    return_g(pa, 1)
    own_g(pa)
    send_g(pa, 0, 1)

    @pl.when(edge)
    def _():
        send_qkv(1, NZ, NT)

    take_g(pa, 1)
    take_g(pa, 2)
    send_g(pa, 1, 2)
    arrived(xbuf.at[far, pl.ds(0, hf)], xh_recv.at[0])
    arrived(xbuf.at[far, pl.ds(hf, hf)], xh_recv.at[1])
    return_g(pa, 2)
    take_g(pa, 3)
    send_g(pa, 3, 1)
    arrived(rcv.at[:, parts[0]], qkv_r.at[0])
    attend(0)
    arrived(rcv.at[:, parts[1]], qkv_r.at[1])
    attend(1)
    attend(2)
    for step in range(3):
        finish(step)
    for cp in stores:
        cp.wait()

    for cp in sent + to_sib:
        cp.wait_send()

    @pl.when(edge)
    def _():
        for cp in to_mirror + to_inner:
            cp.wait_send()

    for i, hs in enumerate(parts):
        others = snd.at[:, hs, pl.ds(0, NT - 1)]
        pltpu.make_async_copy(others, others, qkv_s.at[i]).wait()
    for step, (ph, lo, n, hs) in enumerate(steps):
        others = ph.gs.at[hs, pl.ds(0, NT - 1)]
        pltpu.make_async_copy(others, others, g_s.at[step]).wait()
        others = ph.os.at[:, hs, pl.ds(0, NT - 1)]
        pltpu.make_async_copy(others, others, o_s.at[step]).wait()


def copy_out(a_ref, b_ref, c_ref, x_ref, y_ref, z_ref, buf, in_sem, out_sem):
    frames = a_ref.shape[0]
    pairs = ((a_ref, x_ref), (b_ref, y_ref), (c_ref, z_ref))
    pieces = [(j, i) for j in range(3) for i in range(frames)]
    loads = [pltpu.make_async_copy(pairs[j][0].at[i], buf.at[j, i], in_sem.at[j * frames + i]) for j, i in pieces]
    stores = [pltpu.make_async_copy(buf.at[j, i], pairs[j][1].at[i], out_sem.at[j * frames + i]) for j, i in pieces]
    for cp in loads:
        cp.start()
    for load, store in zip(loads, stores):
        load.wait()
        store.start()
    for cp in stores:
        cp.wait()


def body(queries, key_states, value_states, out_grad, out_proj):
    frames, pos, heads, size = queries.shape
    wrows, width = out_proj.shape
    hbm = pl.BlockSpec(memory_space=pltpu.HBM)
    dma = pltpu.SemaphoreType.DMA

    def turn(a):
        return jnp.transpose(a, (0, 2, 1, 3))

    def phase(count):
        n = NX * count
        return [pltpu.VMEM(shape, BF16) for shape in (
            (n, pos, frames, size), (n, pos, frames, size), (n, NT, frames, size),
            (3, n, NT, frames, size), (3, n, pos, frames, size))]

    outs = pl.pallas_call(
        kernel,
        out_shape=[jax.ShapeDtypeStruct((frames, heads, pos, size), BF16)] * 3,
        in_specs=[hbm] * 5,
        out_specs=[hbm] * 3,
        scratch_shapes=[
            pltpu.VMEM((3, frames, heads, pos, size), BF16),
            pltpu.VMEM((NYH * NC * wrows, width), BF16),
            pltpu.VMEM((NX, frames, pos, width), BF16),
            pltpu.VMEM((3, heads, pos, frames, size), BF16),
            pltpu.VMEM((3, heads, NT, frames, size), BF16),
            *phase(heads // NX),
            pltpu.VMEM((3, frames, heads, pos, size), BF16),
            dma((5,)), dma((2 * NE,)), dma((NE + 1,)), dma((NE + 1,)), dma((NE,)),
            dma((4,)), dma((2,)), dma((2,)), dma((3,)), dma((3,)), dma((3 * NX,)),
            dma((2,)), dma((2,)), dma((3,)), dma((3,)), dma((3,)), dma((3,)),
        ],
        compiler_params=pltpu.CompilerParams(
            collective_id=0, has_side_effects=True, vmem_limit_bytes=60 << 20),
    )(turn(queries), turn(key_states), turn(value_states), out_grad, out_proj)
    outs = pl.pallas_call(
        copy_out,
        out_shape=[jax.ShapeDtypeStruct((frames, heads, pos, size), BF16)] * 3,
        in_specs=[hbm] * 3,
        out_specs=[hbm] * 3,
        scratch_shapes=[pltpu.VMEM((3, frames, heads, pos, size), BF16), dma((3 * frames,)), dma((3 * frames,))],
        compiler_params=pltpu.CompilerParams(vmem_limit_bytes=60 << 20),
    )(*outs)
    return tuple(turn(o) for o in outs)


def solution(mesh):
    return jax.shard_map(
        body,
        mesh=mesh,
        in_specs=(
            P("tm", "fsdp", None, None),
            P("tm", "fsdp", None, None),
            P("tm", "fsdp", None, None),
            P("tm", "fsdp", None),
            P("fsdp", None),
        ),
        out_specs=(
            P("tm", "fsdp", None, None),
            P("tm", "fsdp", None, None),
            P("tm", "fsdp", None, None),
        ),
        check_vma=False,
    )
```

```python
import jax
import jax.numpy as jnp
from jax import lax
from jax.experimental import pallas as pl
from jax.experimental.pallas import tpu as pltpu
from jax.sharding import PartitionSpec as P

MESH = pl.DeviceIdType.MESH
F32 = jnp.float32
BF16 = jnp.bfloat16

NX, NYH, NC = 4, 2, 2
NYL, NZ = 4, 8
NT = NYL * NZ

NE = 6


def mm(a, b, ca, cb):
    return lax.dot_general(a, b, (((ca,), (cb,)), ((), ())), preferred_element_type=F32)


def kernel(q_ref, k_ref, v_ref, x_ref, w_ref, dq_ref, dk_ref, dv_ref,
           qin, wbuf, xbuf, snd, rcv, gst_a, gs_a, gr_a, os_a, or_a,
           in_sem, w_send, sib_send, sib_recv, e_recv, x_send, x_recv, xh_recv,
           gx_send, gx_recv, qkv_s, qkv_r, g_s, g_r, o_s, o_r):
    t = lax.axis_index("tm")
    f = lax.axis_index("fsdp")
    yl, z = t // NZ, t % NZ
    x, yh, c = f // (NYH * NC), (f // NC) % NYH, f % NC
    frames, heads, pos, size = q_ref.shape
    rows = frames * pos
    group = heads // NX
    wrows = w_ref.shape[0]
    part = wrows // NE
    scale = size ** (-0.5)

    def fs(xx, yy, cc):
        return xx * (NYH * NC) + yy * NC + cc

    right, left, far = (x + 1) % NX, (x + NX - 1) % NX, (x + 2) % NX
    oh = 1 - yh
    sib = (t, fs(x, yh, 1 - c))

    def along_x(xx):
        return (t, fs(xx, yh, c))

    mirror = ((NYL - 1 - yl) * NZ + z, fs(x, oh, c))
    edge = jnp.logical_or(yl == 0, yl == NYL - 1)
    inner = (jnp.where(yl == 0, 1, NYL - 2) * NZ + z, f)

    def peer(d):
        away = d - NZ
        dy = jnp.where(d < NZ, 0, 1 + away % (NYL - 1))
        dz = jnp.where(d < NZ, 5 * d, 5 * (away // (NYL - 1)))
        return ((yl + dy) % NYL) * NZ + (z + dz) % NZ

    def block(yy, cc, i=0, n=NE):
        start = pl.multiple_of((yy * NC + cc) * wrows + i * part, 8)
        return wbuf.at[pl.ds(start, n * part), :]

    loads = [pltpu.make_async_copy(src, qin.at[i], in_sem.at[i])
             for i, src in enumerate((q_ref, k_ref, v_ref))]
    loads.append(pltpu.make_async_copy(w_ref, block(yh, c), in_sem.at[3]))
    loads.append(pltpu.make_async_copy(x_ref, xbuf.at[x], in_sem.at[4]))
    for cp in loads:
        cp.start()

    barrier = pltpu.get_barrier_semaphore()

    @pl.loop(1, NT)
    def _(d):
        pl.semaphore_signal(barrier, inc=1, device_id=(peer(d), f), device_id_type=MESH)

    others = (sib, along_x(right), along_x(left), along_x(far), mirror)
    for other in others:
        pl.semaphore_signal(barrier, inc=1, device_id=other, device_id_type=MESH)
    ri = lax.broadcasted_iota(jnp.int32, (rows, rows), 0)
    ci = lax.broadcasted_iota(jnp.int32, (rows, rows), 1)
    to_pos = ((ri % frames) * pos + ri // frames == ci).astype(F32).astype(BF16)
    to_frame = ((ri % pos) * frames + ri // pos == ci).astype(F32).astype(BF16)

    snd_v = snd.reshape(3, heads, rows, size)
    rcv_v = rcv.reshape(3, heads, NT * frames, size)

    for cp in loads[:3]:
        cp.wait()

    order = (x, right, left, far)

    def permute(xs):
        @pl.loop(0, group)
        def _(j):
            for r in xs:
                for i in range(3):
                    src = qin[i, :, order[r] * group + j].reshape(rows, size)
                    snd_v[i, r * group + j] = mm(to_pos, src, 1, 0).astype(BF16)

    permute((0,))

    pl.semaphore_wait(barrier, NT - 1 + len(others))

    def rcopy(src, dst, ssem, rsem, dev):
        return pltpu.make_async_remote_copy(
            src_ref=src, dst_ref=dst, send_sem=ssem, recv_sem=rsem,
            device_id=dev, device_id_type=MESH)

    def arrived(ref, sem):
        pltpu.make_async_copy(ref, ref, sem).wait()

    sent = []

    def send(src, dst, ssem, rsem, dev):
        cp = rcopy(src, dst, ssem, rsem, dev)
        cp.start()
        sent.append(cp)

    to_mirror = [
        rcopy(w_ref.at[pl.ds(i * part, part), :], block(yh, c, i, 1), w_send.at[i], e_recv.at[i], mirror)
        for i in range(NE)
    ]
    to_inner = [
        rcopy(block(oh, c, i, 1), block(oh, c, i, 1), w_send.at[NE + i], e_recv.at[i], inner)
        for i in range(NE)
    ]
    to_sib = [
        rcopy(block(oh, c, i, 1), block(oh, c, i, 1), sib_send.at[i], sib_recv.at[i], sib)
        for i in range(NE)
    ]

    @pl.when(edge)
    def _():
        for cp in to_mirror:
            cp.start()

    send(x_ref, xbuf.at[x], x_send.at[0], x_recv.at[0], along_x(right))
    send(x_ref, xbuf.at[x], x_send.at[1], x_recv.at[1], along_x(left))
    send(w_ref, block(yh, c), sib_send.at[NE], sib_recv.at[NE], sib)

    parts = (pl.ds(0, group), pl.ds(group, heads - group))
    def keep_qkv(i):
        hs = parts[i]
        pltpu.make_async_copy(snd.at[:, hs, t], rcv.at[:, hs, t], qkv_r.at[i]).start()

    def send_qkv(i, lo, hi):
        hs = parts[i]

        @pl.loop(lo, hi)
        def _(d):
            p = peer(d)
            rcopy(snd.at[:, hs, p], rcv.at[:, hs, t], qkv_s.at[i], qkv_r.at[i], (p, f)).start()

    keep_qkv(0)
    send_qkv(0, 1, NZ)

    @pl.when(jnp.logical_not(edge))
    def _():
        send_qkv(0, NZ, NT)

    permute((1, 2, 3))
    keep_qkv(1)
    send_qkv(1, 1, NZ)

    @pl.when(edge)
    def _():
        for i in range(NE):
            arrived(block(oh, c, i, 1), e_recv.at[i])
            to_inner[i].start()
            to_sib[i].start()

        send_qkv(0, NZ, NT)

    @pl.when(jnp.logical_not(edge))
    def _():
        send_qkv(1, NZ, NT)


    class Phase:
        def __init__(self, gst, gs, gr, os, orr, count, head, sems):
            n = NX * count
            self.gst, self.gs, self.gr, self.os, self.orr = gst, gs, gr, os, orr
            self.gst_v = gst.reshape(NX * count, rows, size)
            self.gs_v = gs.reshape(n, rows, size)
            self.gr_v = gr.reshape(n, NT * frames, size)
            self.os_v = os.reshape(3, n, NT * frames, size)
            self.orr_v = orr.reshape(3, n, rows, size)
            self.count, self.head, self.sems = count, head, sems

    pa = Phase(gst_a, gs_a, gr_a, os_a, or_a, group, 0, 0)

    def project(ph, xx):
        acc = mm(xbuf[xx].reshape(rows, -1), wbuf[...], 1, 1).astype(BF16)
        return mm(to_pos, acc, 1, 0).astype(BF16)

    def own_g(ph):
        acc = project(ph, x)
        for j in range(ph.count):
            ph.gs_v[j] = acc[:, j * size:(j + 1) * size]

    back = (2, 1, 3)

    def return_g(ph, i):
        xx = order[i + 1]
        acc = project(ph, xx)
        for j in range(ph.count):
            ph.gst_v[i * ph.count + j] = acc[:, j * size:(j + 1) * size]
        send(ph.gst.at[pl.ds(i * ph.count, ph.count)], ph.gs.at[pl.ds(back[i] * ph.count, ph.count)],
             gx_send.at[ph.sems + i], gx_recv.at[ph.sems + back[i] - 1], along_x(xx))

    def take_g(ph, slot):
        arrived(ph.gs.at[pl.ds(slot * ph.count, ph.count)], gx_recv.at[ph.sems + slot - 1])

    steps = []

    def send_g(ph, lo, n):
        step = len(steps)
        hs = pl.ds(lo * ph.count, n * ph.count)
        steps.append((ph, lo, n, hs))
        pltpu.make_async_copy(ph.gs.at[hs, t], ph.gr.at[hs, t], g_r.at[step]).start()

        @pl.loop(1, NT)
        def _(d):
            p = peer(d)
            rcopy(ph.gs.at[hs, p], ph.gr.at[hs, t], g_s.at[step], g_r.at[step], (p, f)).start()

    def attend(step):
        ph, lo, n, hs = steps[step]
        arrived(ph.gr.at[hs], g_r.at[step])
        for i in range(lo, lo + n):
            for j in range(ph.count):
                h = m = i * ph.count + j
                q, k, v, g = rcv_v[0, h], rcv_v[1, h], rcv_v[2, h], ph.gr_v[m]
                s = mm(k, q, 1, 1) * scale
                e = jnp.exp(s - jnp.max(s, axis=0, keepdims=True))
                probs = e * (1.0 / jnp.sum(e, axis=0, keepdims=True))
                pb16 = probs.astype(BF16)
                dp = mm(v, g, 1, 1)
                delta = jnp.sum(pb16.astype(F32) * dp, axis=0, keepdims=True)
                ds = (probs * (dp - delta)).astype(BF16)
                ph.os_v[0, m] = (mm(ds, k, 0, 0) * scale).astype(BF16)
                ph.os_v[1, m] = (mm(ds, q, 1, 0) * scale).astype(BF16)
                ph.os_v[2, m] = mm(pb16, g, 1, 0).astype(BF16)
        pltpu.make_async_copy(ph.os.at[:, hs, t], ph.orr.at[:, hs, t], o_r.at[step]).start()

        @pl.loop(1, NT)
        def _(d):
            p = peer(d)
            rcopy(ph.os.at[:, hs, p], ph.orr.at[:, hs, t], o_s.at[step], o_r.at[step], (p, f)).start()

    def finish(step):
        ph, lo, n, hs = steps[step]
        arrived(ph.orr.at[:, hs], o_r.at[step])
        for j, ref in enumerate((dq_ref, dk_ref, dv_ref)):
            for i in range(lo, lo + n):
                for u in range(ph.count):
                    ref[:, order[i] * group + ph.head + u] = mm(
                        to_frame, ph.orr_v[j, i * ph.count + u], 1, 0).astype(BF16).reshape(frames, pos, size)

    @pl.when(jnp.logical_not(edge))
    def _():
        for i in range(NE):
            arrived(block(oh, c, i, 1), e_recv.at[i])
            to_sib[i].start()

    hf = frames // 2
    arrived(xbuf.at[left], x_recv.at[0])
    low = xbuf.at[left, pl.ds(0, hf)]
    send(low, low, x_send.at[2], xh_recv.at[0], along_x(right))
    arrived(xbuf.at[right], x_recv.at[1])
    high = xbuf.at[right, pl.ds(hf, hf)]
    send(high, high, x_send.at[3], xh_recv.at[1], along_x(left))

    loads[3].wait()
    loads[4].wait()
    arrived(block(yh, 1 - c), sib_recv.at[NE])
    for i in range(NE):
        arrived(block(oh, 1 - c, i, 1), sib_recv.at[i])
    return_g(pa, 0)
    return_g(pa, 1)
    own_g(pa)
    send_g(pa, 0, 1)

    @pl.when(edge)
    def _():
        send_qkv(1, NZ, NT)

    take_g(pa, 1)
    take_g(pa, 2)
    send_g(pa, 1, 2)
    arrived(xbuf.at[far, pl.ds(0, hf)], xh_recv.at[0])
    arrived(xbuf.at[far, pl.ds(hf, hf)], xh_recv.at[1])
    return_g(pa, 2)
    take_g(pa, 3)
    send_g(pa, 3, 1)
    arrived(rcv.at[:, parts[0]], qkv_r.at[0])
    attend(0)
    arrived(rcv.at[:, parts[1]], qkv_r.at[1])
    attend(1)
    attend(2)
    for step in range(3):
        finish(step)
    for cp in sent + to_sib:
        cp.wait_send()

    @pl.when(edge)
    def _():
        for cp in to_mirror + to_inner:
            cp.wait_send()

    for i, hs in enumerate(parts):
        others = snd.at[:, hs, pl.ds(0, NT - 1)]
        pltpu.make_async_copy(others, others, qkv_s.at[i]).wait()
    for step, (ph, lo, n, hs) in enumerate(steps):
        others = ph.gs.at[hs, pl.ds(0, NT - 1)]
        pltpu.make_async_copy(others, others, g_s.at[step]).wait()
        others = ph.os.at[:, hs, pl.ds(0, NT - 1)]
        pltpu.make_async_copy(others, others, o_s.at[step]).wait()


def copy_out(a_ref, b_ref, c_ref, x_ref, y_ref, z_ref, sem):
    frames = a_ref.shape[0]
    copies = [
        pltpu.make_async_copy(src.at[i], dst.at[i], sem.at[j * frames + i])
        for j, (src, dst) in enumerate(((a_ref, x_ref), (b_ref, y_ref), (c_ref, z_ref)))
        for i in range(frames)
    ]
    for cp in copies:
        cp.start()
    for cp in copies:
        cp.wait()


def body(queries, key_states, value_states, out_grad, out_proj):
    frames, pos, heads, size = queries.shape
    wrows, width = out_proj.shape
    hbm = pl.BlockSpec(memory_space=pltpu.HBM)
    vmem = pl.BlockSpec(memory_space=pltpu.VMEM)
    dma = pltpu.SemaphoreType.DMA

    def turn(a):
        return jnp.transpose(a, (0, 2, 1, 3))

    def phase(count):
        n = NX * count
        return [pltpu.VMEM(shape, BF16) for shape in (
            (n, pos, frames, size), (n, pos, frames, size), (n, NT, frames, size),
            (3, n, NT, frames, size), (3, n, pos, frames, size))]

    outs = pl.pallas_call(
        kernel,
        out_shape=[jax.ShapeDtypeStruct((frames, heads, pos, size), BF16)] * 3,
        in_specs=[hbm] * 5,
        out_specs=[vmem] * 3,
        scratch_shapes=[
            pltpu.VMEM((3, frames, heads, pos, size), BF16),
            pltpu.VMEM((NYH * NC * wrows, width), BF16),
            pltpu.VMEM((NX, frames, pos, width), BF16),
            pltpu.VMEM((3, heads, pos, frames, size), BF16),
            pltpu.VMEM((3, heads, NT, frames, size), BF16),
            *phase(heads // NX),
            dma((5,)), dma((2 * NE,)), dma((NE + 1,)), dma((NE + 1,)), dma((NE,)),
            dma((4,)), dma((2,)), dma((2,)), dma((3,)), dma((3,)),
            dma((2,)), dma((2,)), dma((3,)), dma((3,)), dma((3,)), dma((3,)),
        ],
        compiler_params=pltpu.CompilerParams(
            collective_id=0, has_side_effects=True, vmem_limit_bytes=40 << 20),
    )(*[pltpu.with_memory_space_constraint(a, pltpu.HBM)
        for a in (turn(queries), turn(key_states), turn(value_states), out_grad, out_proj)])
    outs = pl.pallas_call(
        copy_out,
        out_shape=[jax.ShapeDtypeStruct((frames, heads, pos, size), BF16)] * 3,
        in_specs=[vmem] * 3,
        out_specs=[hbm] * 3,
        scratch_shapes=[dma((3 * frames,))],
        compiler_params=pltpu.CompilerParams(vmem_limit_bytes=40 << 20),
    )(*outs)
    return tuple(turn(o) for o in outs)


def solution(mesh):
    return jax.shard_map(
        body,
        mesh=mesh,
        in_specs=(
            P("tm", "fsdp", None, None),
            P("tm", "fsdp", None, None),
            P("tm", "fsdp", None, None),
            P("tm", "fsdp", None),
            P("fsdp", None),
        ),
        out_specs=(
            P("tm", "fsdp", None, None),
            P("tm", "fsdp", None, None),
            P("tm", "fsdp", None, None),
        ),
        check_vma=False,
    )
```

```python
import jax
import jax.numpy as jnp
from jax import lax
from jax.experimental import pallas as pl
from jax.experimental.pallas import tpu as pltpu
from jax.sharding import PartitionSpec as P

MESH = pl.DeviceIdType.MESH
F32 = jnp.float32
BF16 = jnp.bfloat16

NX, NYH, NC = 4, 2, 2
NYL, NZ = 4, 8
NT = NYL * NZ

NE = 6


def mm(a, b, ca, cb):
    return lax.dot_general(a, b, (((ca,), (cb,)), ((), ())), preferred_element_type=F32)


def kernel(q_ref, k_ref, v_ref, x_ref, w_ref, dq_ref, dk_ref, dv_ref,
           qin, wbuf, xbuf, snd, rcv, gst_a, gs_a, gr_a, os_a, or_a,
           in_sem, w_send, sib_send, sib_recv, e_recv, x_send, x_recv, xh_recv,
           gx_send, gx_recv, qkv_s, qkv_r, g_s, g_r, o_s, o_r):
    t = lax.axis_index("tm")
    f = lax.axis_index("fsdp")
    yl, z = t // NZ, t % NZ
    x, yh, c = f // (NYH * NC), (f // NC) % NYH, f % NC
    frames, heads, pos, size = q_ref.shape
    rows = frames * pos
    group = heads // NX
    wrows = w_ref.shape[0]
    part = wrows // NE
    scale = size ** (-0.5)

    def fs(xx, yy, cc):
        return xx * (NYH * NC) + yy * NC + cc

    right, left, far = (x + 1) % NX, (x + NX - 1) % NX, (x + 2) % NX
    oh = 1 - yh
    sib = (t, fs(x, yh, 1 - c))

    def along_x(xx):
        return (t, fs(xx, yh, c))

    mirror = ((NYL - 1 - yl) * NZ + z, fs(x, oh, c))
    edge = jnp.logical_or(yl == 0, yl == NYL - 1)
    inner = (jnp.where(yl == 0, 1, NYL - 2) * NZ + z, f)

    def peer(d):
        away = d - NZ
        dy = jnp.where(d < NZ, 0, 1 + away % (NYL - 1))
        dz = jnp.where(d < NZ, 5 * d, 5 * (away // (NYL - 1)))
        return ((yl + dy) % NYL) * NZ + (z + dz) % NZ

    def block(yy, cc, i=0, n=NE):
        start = pl.multiple_of((yy * NC + cc) * wrows + i * part, 8)
        return wbuf.at[pl.ds(start, n * part), :]

    loads = [pltpu.make_async_copy(src, qin.at[i], in_sem.at[i])
             for i, src in enumerate((q_ref, k_ref, v_ref))]
    loads.append(pltpu.make_async_copy(w_ref, block(yh, c), in_sem.at[3]))
    loads.append(pltpu.make_async_copy(x_ref, xbuf.at[x], in_sem.at[4]))
    for cp in loads:
        cp.start()

    barrier = pltpu.get_barrier_semaphore()

    @pl.loop(1, NT)
    def _(d):
        pl.semaphore_signal(barrier, inc=1, device_id=(peer(d), f), device_id_type=MESH)

    others = (sib, along_x(right), along_x(left), along_x(far), mirror)
    for other in others:
        pl.semaphore_signal(barrier, inc=1, device_id=other, device_id_type=MESH)
    ri = lax.broadcasted_iota(jnp.int32, (rows, rows), 0)
    ci = lax.broadcasted_iota(jnp.int32, (rows, rows), 1)
    to_pos = ((ri % frames) * pos + ri // frames == ci).astype(F32).astype(BF16)
    to_frame = ((ri % pos) * frames + ri // pos == ci).astype(F32).astype(BF16)

    snd_v = snd.reshape(3, heads, rows, size)
    rcv_v = rcv.reshape(3, heads, NT * frames, size)

    for cp in loads[:3]:
        cp.wait()

    order = (x, right, left, far)

    def permute(xs):
        @pl.loop(0, group)
        def _(j):
            for r in xs:
                for i in range(3):
                    src = qin[i, :, order[r] * group + j].reshape(rows, size)
                    snd_v[i, r * group + j] = mm(to_pos, src, 1, 0).astype(BF16)

    permute((0, 1))

    pl.semaphore_wait(barrier, NT - 1 + len(others))

    def rcopy(src, dst, ssem, rsem, dev):
        return pltpu.make_async_remote_copy(
            src_ref=src, dst_ref=dst, send_sem=ssem, recv_sem=rsem,
            device_id=dev, device_id_type=MESH)

    def arrived(ref, sem):
        pltpu.make_async_copy(ref, ref, sem).wait()

    sent = []

    def send(src, dst, ssem, rsem, dev):
        cp = rcopy(src, dst, ssem, rsem, dev)
        cp.start()
        sent.append(cp)

    to_mirror = [
        rcopy(w_ref.at[pl.ds(i * part, part), :], block(yh, c, i, 1), w_send.at[i], e_recv.at[i], mirror)
        for i in range(NE)
    ]
    to_inner = [
        rcopy(block(oh, c, i, 1), block(oh, c, i, 1), w_send.at[NE + i], e_recv.at[i], inner)
        for i in range(NE)
    ]
    to_sib = [
        rcopy(block(oh, c, i, 1), block(oh, c, i, 1), sib_send.at[i], sib_recv.at[i], sib)
        for i in range(NE)
    ]

    @pl.when(edge)
    def _():
        for cp in to_mirror:
            cp.start()

    send(x_ref, xbuf.at[x], x_send.at[0], x_recv.at[0], along_x(right))
    send(x_ref, xbuf.at[x], x_send.at[1], x_recv.at[1], along_x(left))
    send(w_ref, block(yh, c), sib_send.at[NE], sib_recv.at[NE], sib)

    parts = (pl.ds(0, 2 * group), pl.ds(2 * group, heads - 2 * group))
    def keep_qkv(i):
        hs = parts[i]
        pltpu.make_async_copy(snd.at[:, hs, t], rcv.at[:, hs, t], qkv_r.at[i]).start()

    def send_qkv(i, lo, hi):
        hs = parts[i]

        @pl.loop(lo, hi)
        def _(d):
            p = peer(d)
            rcopy(snd.at[:, hs, p], rcv.at[:, hs, t], qkv_s.at[i], qkv_r.at[i], (p, f)).start()

    keep_qkv(0)
    send_qkv(0, 1, NZ)

    @pl.when(jnp.logical_not(edge))
    def _():
        send_qkv(0, NZ, NT)

    permute((2, 3))
    keep_qkv(1)
    send_qkv(1, 1, NZ)

    @pl.when(edge)
    def _():
        for i in range(NE):
            arrived(block(oh, c, i, 1), e_recv.at[i])
            to_inner[i].start()
            to_sib[i].start()

        send_qkv(0, NZ, NT)

    @pl.when(jnp.logical_not(edge))
    def _():
        send_qkv(1, NZ, NT)


    class Phase:
        def __init__(self, gst, gs, gr, os, orr, count, head, sems):
            n = NX * count
            self.gst, self.gs, self.gr, self.os, self.orr = gst, gs, gr, os, orr
            self.gst_v = gst.reshape(NX * count, rows, size)
            self.gs_v = gs.reshape(n, rows, size)
            self.gr_v = gr.reshape(n, NT * frames, size)
            self.os_v = os.reshape(3, n, NT * frames, size)
            self.orr_v = orr.reshape(3, n, rows, size)
            self.count, self.head, self.sems = count, head, sems

    pa = Phase(gst_a, gs_a, gr_a, os_a, or_a, group, 0, 0)

    def project(ph, xx):
        acc = mm(xbuf[xx].reshape(rows, -1), wbuf[...], 1, 1).astype(BF16)
        return mm(to_pos, acc, 1, 0).astype(BF16)

    def own_g(ph):
        acc = project(ph, x)
        for j in range(ph.count):
            ph.gs_v[j] = acc[:, j * size:(j + 1) * size]

    back = (2, 1, 3)

    def return_g(ph, i):
        xx = order[i + 1]
        acc = project(ph, xx)
        for j in range(ph.count):
            ph.gst_v[i * ph.count + j] = acc[:, j * size:(j + 1) * size]
        send(ph.gst.at[pl.ds(i * ph.count, ph.count)], ph.gs.at[pl.ds(back[i] * ph.count, ph.count)],
             gx_send.at[ph.sems + i], gx_recv.at[ph.sems + back[i] - 1], along_x(xx))

    def take_g(ph, slot):
        arrived(ph.gs.at[pl.ds(slot * ph.count, ph.count)], gx_recv.at[ph.sems + slot - 1])

    steps = []

    def send_g(ph, lo, n):
        step = len(steps)
        hs = pl.ds(lo * ph.count, n * ph.count)
        steps.append((ph, lo, n, hs))
        pltpu.make_async_copy(ph.gs.at[hs, t], ph.gr.at[hs, t], g_r.at[step]).start()

        @pl.loop(1, NT)
        def _(d):
            p = peer(d)
            rcopy(ph.gs.at[hs, p], ph.gr.at[hs, t], g_s.at[step], g_r.at[step], (p, f)).start()

    def attend(step):
        ph, lo, n, hs = steps[step]
        arrived(ph.gr.at[hs], g_r.at[step])
        for i in range(lo, lo + n):
            for j in range(ph.count):
                h = m = i * ph.count + j
                q, k, v, g = rcv_v[0, h], rcv_v[1, h], rcv_v[2, h], ph.gr_v[m]
                s = mm(k, q, 1, 1) * scale
                e = jnp.exp(s - jnp.max(s, axis=0, keepdims=True))
                probs = e * (1.0 / jnp.sum(e, axis=0, keepdims=True))
                pb16 = probs.astype(BF16)
                dp = mm(v, g, 1, 1)
                delta = jnp.sum(pb16.astype(F32) * dp, axis=0, keepdims=True)
                ds = (probs * (dp - delta)).astype(BF16)
                ph.os_v[0, m] = (mm(ds, k, 0, 0) * scale).astype(BF16)
                ph.os_v[1, m] = (mm(ds, q, 1, 0) * scale).astype(BF16)
                ph.os_v[2, m] = mm(pb16, g, 1, 0).astype(BF16)
        pltpu.make_async_copy(ph.os.at[:, hs, t], ph.orr.at[:, hs, t], o_r.at[step]).start()

        @pl.loop(1, NT)
        def _(d):
            p = peer(d)
            rcopy(ph.os.at[:, hs, p], ph.orr.at[:, hs, t], o_s.at[step], o_r.at[step], (p, f)).start()

    def finish(step):
        ph, lo, n, hs = steps[step]
        arrived(ph.orr.at[:, hs], o_r.at[step])
        for j, ref in enumerate((dq_ref, dk_ref, dv_ref)):
            for i in range(lo, lo + n):
                for u in range(ph.count):
                    ref[:, order[i] * group + ph.head + u] = mm(
                        to_frame, ph.orr_v[j, i * ph.count + u], 1, 0).astype(BF16).reshape(frames, pos, size)

    @pl.when(jnp.logical_not(edge))
    def _():
        for i in range(NE):
            arrived(block(oh, c, i, 1), e_recv.at[i])
            to_sib[i].start()

    hf = frames // 2
    arrived(xbuf.at[left], x_recv.at[0])
    low = xbuf.at[left, pl.ds(0, hf)]
    send(low, low, x_send.at[2], xh_recv.at[0], along_x(right))
    arrived(xbuf.at[right], x_recv.at[1])
    high = xbuf.at[right, pl.ds(hf, hf)]
    send(high, high, x_send.at[3], xh_recv.at[1], along_x(left))

    loads[3].wait()
    loads[4].wait()
    arrived(block(yh, 1 - c), sib_recv.at[NE])
    for i in range(NE):
        arrived(block(oh, 1 - c, i, 1), sib_recv.at[i])
    return_g(pa, 0)
    return_g(pa, 1)
    own_g(pa)
    send_g(pa, 0, 1)

    @pl.when(edge)
    def _():
        send_qkv(1, NZ, NT)

    take_g(pa, 1)
    take_g(pa, 2)
    send_g(pa, 1, 2)
    arrived(xbuf.at[far, pl.ds(0, hf)], xh_recv.at[0])
    arrived(xbuf.at[far, pl.ds(hf, hf)], xh_recv.at[1])
    return_g(pa, 2)
    take_g(pa, 3)
    send_g(pa, 3, 1)
    arrived(rcv.at[:, parts[0]], qkv_r.at[0])
    attend(0)
    arrived(rcv.at[:, parts[1]], qkv_r.at[1])
    attend(1)
    attend(2)
    for step in range(3):
        finish(step)
    for cp in sent + to_sib:
        cp.wait_send()

    @pl.when(edge)
    def _():
        for cp in to_mirror + to_inner:
            cp.wait_send()

    for i, hs in enumerate(parts):
        others = snd.at[:, hs, pl.ds(0, NT - 1)]
        pltpu.make_async_copy(others, others, qkv_s.at[i]).wait()
    for step, (ph, lo, n, hs) in enumerate(steps):
        others = ph.gs.at[hs, pl.ds(0, NT - 1)]
        pltpu.make_async_copy(others, others, g_s.at[step]).wait()
        others = ph.os.at[:, hs, pl.ds(0, NT - 1)]
        pltpu.make_async_copy(others, others, o_s.at[step]).wait()


def copy_out(a_ref, b_ref, c_ref, x_ref, y_ref, z_ref, sem):
    frames = a_ref.shape[0]
    copies = [
        pltpu.make_async_copy(src.at[i], dst.at[i], sem.at[j * frames + i])
        for j, (src, dst) in enumerate(((a_ref, x_ref), (b_ref, y_ref), (c_ref, z_ref)))
        for i in range(frames)
    ]
    for cp in copies:
        cp.start()
    for cp in copies:
        cp.wait()


def body(queries, key_states, value_states, out_grad, out_proj):
    frames, pos, heads, size = queries.shape
    wrows, width = out_proj.shape
    hbm = pl.BlockSpec(memory_space=pltpu.HBM)
    vmem = pl.BlockSpec(memory_space=pltpu.VMEM)
    dma = pltpu.SemaphoreType.DMA

    def turn(a):
        return jnp.transpose(a, (0, 2, 1, 3))

    def phase(count):
        n = NX * count
        return [pltpu.VMEM(shape, BF16) for shape in (
            (n, pos, frames, size), (n, pos, frames, size), (n, NT, frames, size),
            (3, n, NT, frames, size), (3, n, pos, frames, size))]

    outs = pl.pallas_call(
        kernel,
        out_shape=[jax.ShapeDtypeStruct((frames, heads, pos, size), BF16)] * 3,
        in_specs=[hbm] * 5,
        out_specs=[vmem] * 3,
        scratch_shapes=[
            pltpu.VMEM((3, frames, heads, pos, size), BF16),
            pltpu.VMEM((NYH * NC * wrows, width), BF16),
            pltpu.VMEM((NX, frames, pos, width), BF16),
            pltpu.VMEM((3, heads, pos, frames, size), BF16),
            pltpu.VMEM((3, heads, NT, frames, size), BF16),
            *phase(heads // NX),
            dma((5,)), dma((2 * NE,)), dma((NE + 1,)), dma((NE + 1,)), dma((NE,)),
            dma((4,)), dma((2,)), dma((2,)), dma((3,)), dma((3,)),
            dma((2,)), dma((2,)), dma((3,)), dma((3,)), dma((3,)), dma((3,)),
        ],
        compiler_params=pltpu.CompilerParams(
            collective_id=0, has_side_effects=True, vmem_limit_bytes=40 << 20),
    )(*[pltpu.with_memory_space_constraint(a, pltpu.HBM)
        for a in (turn(queries), turn(key_states), turn(value_states), out_grad, out_proj)])
    outs = pl.pallas_call(
        copy_out,
        out_shape=[jax.ShapeDtypeStruct((frames, heads, pos, size), BF16)] * 3,
        in_specs=[vmem] * 3,
        out_specs=[hbm] * 3,
        scratch_shapes=[dma((3 * frames,))],
        compiler_params=pltpu.CompilerParams(vmem_limit_bytes=40 << 20),
    )(*outs)
    return tuple(turn(o) for o in outs)


def solution(mesh):
    return jax.shard_map(
        body,
        mesh=mesh,
        in_specs=(
            P("tm", "fsdp", None, None),
            P("tm", "fsdp", None, None),
            P("tm", "fsdp", None, None),
            P("tm", "fsdp", None),
            P("fsdp", None),
        ),
        out_specs=(
            P("tm", "fsdp", None, None),
            P("tm", "fsdp", None, None),
            P("tm", "fsdp", None, None),
        ),
        check_vma=False,
    )
```
